32 devices in a mesh: ctx: 8 (over z, x), tp: 4 (over y, core).
Axes of the slice: x: 2, y: 2, z: 4, core: 2. Of those that a mesh axis runs over, the one named last changes fastest.
Arguments:
- queries: bfloat16 [2048, 2560], P('ctx', 'tp'), may hold values from -5 to 5
- keys: bfloat16 [2048, 2560], P('ctx', 'tp'), may hold values from -5 to 5
- values: bfloat16 [2048, 2560], P('ctx', 'tp'), may hold values from -6 to 6
- block_mask: int32 [16, 16], replicated, may hold values from 0 to 1, as said below
- w_out: bfloat16 [2560, 5120], P('tp'), may hold values from -0.125 to 0.125
Outputs:
- mixed: bfloat16 [2048, 5120], P('ctx', 'tp')
The draws below stay inside these ranges and needn't reach their ends.
Inputs may be any that keep to these rules, and one draw needn't show every extreme that they name: block_mask[b, b] = 1 for every block b. block_mask[i, j] = 0 whenever the ctx indices i // 2 and j // 2 differ by more than 2; where they differ by exactly 2 and i and j have the same position within their devices, block_mask[i, j] = 1.
All inputs are finite; a program needn't handle non-finite values.
Results may differ from the reference program's by a relative error of at most 0.014.
Values may be sent and summed in bfloat16 or wider, within the bound.
A program may use at most 64 MiB of HBM per device.

```python
import jax
import jax.numpy as jnp
from jax import lax

D = 5120
HEADS = 20
HD = 128
BLK = 128
TOK_DEV = 256
TOKENS = 2048
NB = 16
REACH = 2


def query_key_pair(key):
    base = jax.random.fold_in(key, 7)
    key_query, key_key = jax.random.split(base, 2)
    shape = (TOKENS, HEADS * HD)
    query_draw = jax.random.normal(key_query, shape, jnp.float32)
    key_draw = jax.random.normal(key_key, shape, jnp.float32)
    return (jnp.clip(query_draw, -5.0, 5.0), jnp.clip(key_draw, -5.0, 5.0))


def draw_queries(key, part):
    return query_key_pair(key)[0].astype(jnp.bfloat16)


def draw_keys(key, part):
    return query_key_pair(key)[1].astype(jnp.bfloat16)


def draw_block_mask(key, part):
    per_dev = TOK_DEV // BLK
    row_ids = jnp.arange(NB, dtype=jnp.int32)[:, None]
    col_ids = jnp.arange(NB, dtype=jnp.int32)[None, :]
    distance = jnp.abs(row_ids // per_dev - col_ids // per_dev)
    chance = jax.random.randint(jax.random.fold_in(key, 11), (NB, NB), 0, 1000)
    keep = (chance < 900 // (1 + distance)) & (distance <= REACH)
    forced = (distance == REACH) & (row_ids % per_dev == col_ids % per_dev)
    keep = keep | (row_ids == col_ids) | forced
    return keep.astype(jnp.int32)


def levels(own_key, extent, cuts, low, top_value):
    factor_of = 1.0
    for position, blocks in cuts:
        steps = jax.random.uniform(jax.random.fold_in(jax.random.fold_in(own_key, 6), position), (blocks,), jnp.float32, low / len(cuts), top_value / len(cuts))
        factor_of = factor_of * jnp.repeat(jnp.exp(steps), extent[position] // blocks).reshape((-1,) + (1,) * (len(extent) - 1 - position))
    return factor_of


def bell_draw(own_key, extent, scale, bound, cuts=(), held_as=jnp.bfloat16):
    drawn = scale * jax.random.normal(own_key, extent, jnp.float32)
    if cuts:
        drawn = drawn * levels(own_key, extent, cuts, -0.22, 0.18)
    return jnp.clip(drawn, -bound, bound).astype(held_as)


def setup_inputs(seed: int = 0) -> dict:
    streams_of = jax.random.split(jax.random.key(seed), 6)
    queries = draw_queries(jax.random.fold_in(streams_of[5], 71), 0)
    keys = draw_keys(jax.random.fold_in(streams_of[5], 71), 0)
    values = bell_draw(streams_of[2], (TOKENS, HEADS * HD), 1.0, 6.0, ((0, 8), (1, 4)))
    block_mask = draw_block_mask(jax.random.fold_in(streams_of[5], 71), 0)
    w_out = bell_draw(streams_of[4], (HEADS * HD, D), (HEADS * HD) ** -0.5, 0.125, ((0, 4),))
    return {"queries": queries, "keys": keys, "values": values, "block_mask": block_mask, "w_out": w_out}


def reference(queries, keys, values, block_mask, w_out):
    scale = HD ** -0.5
    allowed = jnp.repeat(jnp.repeat(block_mask, BLK, axis=0), BLK, axis=1) > 0
    query_heads = queries.reshape(TOKENS, HEADS, HD)
    key_heads = keys.reshape(TOKENS, HEADS, HD)
    value_heads = values.reshape(TOKENS, HEADS, HD)

    def one_head(head):
        query_one = lax.dynamic_index_in_dim(query_heads, head, 1, keepdims=False)
        key_one = lax.dynamic_index_in_dim(key_heads, head, 1, keepdims=False)
        value_one = lax.dynamic_index_in_dim(value_heads, head, 1, keepdims=False)
        scores = jnp.dot(query_one, key_one.T, preferred_element_type=jnp.float32) * scale
        masked = jnp.where(allowed, scores, jnp.float32(-1e30))
        maxima = jnp.max(masked, axis=1, keepdims=True)
        probs = jnp.where(allowed, jnp.exp(masked - maxima), jnp.float32(0.0))
        totals = jnp.sum(probs, axis=1, keepdims=True)
        summed = jnp.dot(probs.astype(jnp.bfloat16), value_one, preferred_element_type=jnp.float32)
        return summed / totals

    outputs = lax.map(one_head, jnp.arange(HEADS, dtype=jnp.int32))
    attended = jnp.transpose(outputs, (1, 0, 2)).reshape(TOKENS, HEADS * HD).astype(jnp.bfloat16)
    return jnp.dot(attended, w_out, preferred_element_type=jnp.float32).astype(jnp.bfloat16)
```

```python
import functools
import math

import jax
import jax.numpy as jnp
from jax import lax
from jax.experimental import pallas as pl
from jax.experimental.pallas import tpu as pltpu
from jax.sharding import PartitionSpec as P

HD = 128
BLK = 128
MESH = pl.DeviceIdType.MESH
K, V = 0, 1
DOWN, UP = 0, 1
NONE = -1e30


def kernel(
    reach, count, tp_count, chunks,
    mask_ref, q_ref, k_ref, v_ref, w_ref, out_ref,
    q_own, kv_row, kv_col, q_row, q_col, o_row, o_col, got_row, got_col,
    lse_row, lse_col, got_lse_row, got_lse_col, acc, peak, att, att_peer,
    w_own, w_peer, stage_y, recv_y, near, final,
    own_sem, w_sem, wp_send, wp_recv, kvr_send, kvr_recv, kvc_send, kvc_recv,
    qr_send, qr_recv, qc_send, qc_recv, or_send, or_recv, oc_send, oc_recv,
    lr_send, lr_recv, lc_send, lc_recv, att_send, att_recv, y_send, y_recv, out_sem,
):
    tok, cols = q_own.shape
    heads = cols // HD
    per = tok // BLK
    chips = tp_count // 2
    out_cols = out_ref.shape[1]
    width = out_cols // chunks
    half = heads // 2
    odd = heads % 2
    middle = half
    ctx = lax.axis_index("ctx")
    t = lax.axis_index("tp")
    inner = lax.rem(ctx, reach)
    core = lax.rem(t, 2)
    chip = t // 2
    partner = chip * 2 + 1 - core
    factor = jnp.float32(HD ** (-0.5) * math.log2(math.e))

    def tp_of(jy, which):
        return lax.rem(chip + jy, chips) * 2 + which

    def each_peer(fn):
        if reach == 2:
            fn(1 - inner)
        elif reach > 2:
            def step(j, carry):
                fn(lax.rem(inner + j, reach))
                return carry
            lax.fori_loop(1, reach, step, 0)

    def in_row(p):
        return ctx - inner + p

    def outer_of(d):
        return ctx + (2 * d - 1) * reach

    def inside(c):
        return jnp.logical_and(c >= 0, c < count)

    def each_outer(fn):
        for d in (DOWN, UP):
            @pl.when(inside(outer_of(d)))
            def _(d=d):
                fn(d)

    def lanes(h):
        return slice(h * HD, (h + 1) * HD)

    def rows(r):
        return slice(r * BLK, (r + 1) * BLK)

    def remote(src, dst, send, recv, c, tt):
        return pltpu.make_async_remote_copy(
            src_ref=src, dst_ref=dst, send_sem=send, recv_sem=recv,
            device_id=(c, tt), device_id_type=MESH,
        )

    def kv_row_copy(p, kind, h, slot=None):
        slot = inner if slot is None else slot
        return remote(
            (k_ref, v_ref)[kind].at[:, lanes(h)], kv_row.at[slot, kind, :, lanes(h)],
            kvr_send.at[p, kind, h], kvr_recv.at[slot, kind, h], in_row(p), t,
        )

    def kv_col_copy(d, kind, h, slot=None):
        slot = 1 - d if slot is None else slot
        return remote(
            (k_ref, v_ref)[kind].at[:, lanes(h)], kv_col.at[slot, kind, :, lanes(h)],
            kvc_send.at[d, kind, h], kvc_recv.at[slot, kind, h], outer_of(d), t,
        )

    def group(kind, g):
        if g:
            return slice(middle * HD, (middle + 1) * HD)
        return slice(0, half * HD) if kind == "col" else slice((half + odd) * HD, cols)

    def q_row_copy(p, r, g, slot=None):
        slot = inner if slot is None else slot
        part = (rows(r), group("row", g))
        return remote(
            q_ref.at[part], q_row.at[(slot,) + part],
            qr_send.at[p, r, g], qr_recv.at[slot, r, g], in_row(p), t,
        )

    def q_col_copy(d, r, g, slot=None):
        slot = 1 - d if slot is None else slot
        part = (rows(r), group("col", g))
        return remote(
            q_ref.at[part], q_col.at[(slot,) + part],
            qc_send.at[d, r, g], qc_recv.at[slot, r, g], outer_of(d), t,
        )

    def o_row_copy(p, r, h, slot=None):
        slot = inner if slot is None else slot
        part = (rows(r), lanes(h))
        return remote(
            o_row.at[(p,) + part], got_row.at[(slot,) + part],
            or_send.at[p, r, h], or_recv.at[slot, r, h], in_row(p), t,
        )

    def o_col_copy(d, r, h, slot=None):
        slot = 1 - d if slot is None else slot
        part = (rows(r), lanes(h))
        return remote(
            o_col.at[(d,) + part], got_col.at[(slot,) + part],
            oc_send.at[d, r, h], oc_recv.at[slot, r, h], outer_of(d), t,
        )

    def lse_row_copy(p, r, slot=None):
        slot = inner if slot is None else slot
        return remote(
            lse_row.at[p, r], got_lse_row.at[slot, r],
            lr_send.at[p, r], lr_recv.at[slot, r], in_row(p), t,
        )

    def lse_col_copy(d, r, slot=None):
        slot = 1 - d if slot is None else slot
        return remote(
            lse_col.at[d, r], got_lse_col.at[slot, r],
            lc_send.at[d, r], lc_recv.at[slot, r], outer_of(d), t,
        )

    def weight_copy(jy):
        start = pl.multiple_of(tp_of(jy, 1 - core) * out_cols, out_cols)
        return remote(
            w_ref.at[:, pl.ds(start, out_cols)], w_peer.at[jy],
            wp_send.at[jy], wp_recv.at[jy], ctx, partner,
        )

    def att_copy(r):
        return remote(
            att.at[rows(r), :], att_peer.at[rows(r), :],
            att_send.at[r], att_recv.at[r], ctx, partner,
        )

    def chip_copy(jy, r, k):
        return remote(
            stage_y.at[jy - 1, r, k], recv_y.at[chips - jy - 1, r, k],
            y_send.at[jy - 1, r, k], y_recv.at[chips - jy - 1, r, k], ctx, tp_of(jy, core),
        )

    def out_copy(r, k):
        return pltpu.make_async_copy(
            final.at[r, k], out_ref.at[rows(r), k * width:(k + 1) * width], out_sem.at[r, k]
        )

    own = [
        pltpu.make_async_copy(q_ref, q_own, own_sem.at[0]),
        pltpu.make_async_copy(k_ref, kv_row.at[inner, K], own_sem.at[1]),
        pltpu.make_async_copy(v_ref, kv_row.at[inner, V], own_sem.at[2]),
    ]
    weights = []
    for jy in range(chips):
        start = pl.multiple_of(tp_of(jy, core) * out_cols, out_cols)
        weights.append(pltpu.make_async_copy(
            w_ref.at[:, pl.ds(start, out_cols)], w_own.at[jy], w_sem.at[jy]
        ))

    barrier = pltpu.get_barrier_semaphore()

    def greet(c, tt):
        pl.semaphore_signal(barrier, inc=1, device_id=(c, tt), device_id_type=MESH)

    each_peer(lambda p: greet(in_row(p), t))
    each_outer(lambda d: greet(outer_of(d), t))
    greet(ctx, partner)
    for jy in range(1, chips):
        greet(ctx, tp_of(jy, core))
    outer_count = inside(outer_of(DOWN)).astype(jnp.int32) + inside(outer_of(UP)).astype(jnp.int32)
    pl.semaphore_wait(barrier, reach - 1 + 1 + chips - 1 + outer_count)

    row_heads = list(range(half))
    col_heads = list(range(heads - 1, heads - 1 - half, -1))

    def by_core(which, fn):
        if odd:
            @pl.when(core == which)
            def _():
                fn()

    def start_queries(r):
        each_peer(lambda p: q_row_copy(p, r, 0).start())
        by_core(1, lambda: each_peer(lambda p: q_row_copy(p, r, 1).start()))
        each_outer(lambda d: q_col_copy(d, r, 0).start())
        by_core(0, lambda: each_outer(lambda d: q_col_copy(d, r, 1).start()))

    def start_row_keys(h):
        for kind in (K, V):
            each_peer(lambda p: kv_row_copy(p, kind, h).start())

    def start_col_keys(h):
        def go(d):
            for kind in (K, V):
                kv_col_copy(d, kind, h).start()
        each_outer(go)

    start_queries(0)
    for a, b in zip(row_heads, col_heads):
        start_row_keys(a)
        start_col_keys(b)
    by_core(0, lambda: start_row_keys(middle))
    by_core(1, lambda: start_col_keys(middle))
    for r in range(1, per):
        start_queries(r)
    for copy in own:
        copy.start()
    for jy in list(range(1, chips)) + [0]:
        weight_copy(jy).start()
    for copy in weights[1:] + weights[:1]:
        copy.start()

    for d in (DOWN, UP):
        @pl.when(jnp.logical_not(inside(outer_of(d))))
        def _(d=d):
            kv_col[d] = jnp.zeros(kv_col.shape[1:], kv_col.dtype)
            q_col[d] = jnp.zeros(q_col.shape[1:], q_col.dtype)
            got_col[d] = jnp.zeros(got_col.shape[1:], got_col.dtype)
            got_lse_col[d] = jnp.full(got_lse_col.shape[1:], NONE, jnp.float32)
    lse_row[...] = jnp.zeros_like(lse_row)
    lse_col[...] = jnp.zeros_like(lse_col)

    def bias_of(block, owner):
        owner_in = jnp.clip(owner, 0, count - 1)
        block_in = jnp.clip(block, 0, count * per - 1)
        parts = []
        for b in range(per):
            flag = jnp.where(inside(owner), mask_ref[block_in, owner_in * per + b], 0)
            value = jnp.where(flag > 0, jnp.float32(0.0), jnp.float32(NONE))
            parts.append(jnp.full((1, BLK), value, jnp.float32))
        return parts

    def scores_of(query, pieces):
        key = jnp.concatenate([piece[0] for piece in pieces], axis=0)
        return lax.dot_general(
            query, key, (((1,), (1,)), ((), ())), preferred_element_type=jnp.float32
        )

    def sums_of(weight, pieces):
        value = jnp.concatenate([piece[1] for piece in pieces], axis=0)
        ones = jnp.ones((value.shape[0], HD), jnp.bfloat16)
        return jnp.dot(
            weight, jnp.concatenate([value, ones], axis=1), preferred_element_type=jnp.float32
        )

    def partial(query, block, pieces):
        raw = scores_of(query, pieces)
        weight, tops = [], []
        for a in range(query.shape[0] // BLK):
            bias = jnp.concatenate(
                sum([bias_of(block + a, piece[2]) for piece in pieces], []), axis=1
            )
            scores = raw[rows(a)] + bias
            top = jnp.broadcast_to(jnp.max(scores, axis=1, keepdims=True), (BLK, HD))
            wide = jnp.concatenate([top] * (scores.shape[1] // HD), axis=1)
            weight.append(jnp.exp2((scores - wide) * factor).astype(jnp.bfloat16))
            tops.append(top * factor)
        return sums_of(jnp.concatenate(weight, axis=0), pieces), jnp.concatenate(tops, axis=0)

    def fade(before, after):
        scale = jnp.exp2(before - after)
        return jnp.concatenate([scale, scale], axis=1)

    def partial_row(query, block, h, low, high):
        def step(slot, carry):
            total, top = carry
            more, more_top = partial(query, block, [row_piece(slot, h)])
            best = jnp.maximum(top, more_top)
            return total * fade(top, best) + more * fade(more_top, best), best
        shape = (query.shape[0], HD)
        first = (jnp.zeros((shape[0], 2 * HD), jnp.float32), jnp.full(shape, -1e38, jnp.float32))
        return lax.fori_loop(low, high, step, first)

    def row_piece(slot, h):
        return kv_row[slot, K, :, lanes(h)], kv_row[slot, V, :, lanes(h)], in_row(slot)

    def col_piece(d, h):
        return kv_col[d, K, :, lanes(h)], kv_col[d, V, :, lanes(h)], outer_of(d)

    def keep(h, total, top):
        acc[h] = total
        peak[h] = top

    def own_row(h):
        query = q_own[:, lanes(h)]
        if reach == 2:
            pieces = [row_piece(inner, h), row_piece(1 - inner, h)]
            keep(h, *partial(query, ctx * per, pieces))
        else:
            keep(h, *partial_row(query, ctx * per, h, 0, reach))

    def own_col(h):
        pieces = [row_piece(inner, h), col_piece(DOWN, h), col_piece(UP, h)]
        keep(h, *partial(q_own[:, lanes(h)], ctx * per, pieces))

    def answer(total, top, o_ref, lse_ref, h):
        below = total[:, HD:]
        o_ref[...] = (total[:, :HD] * (1.0 / below)).astype(jnp.bfloat16)
        lse = top + jnp.log(below) * jnp.float32(math.log2(math.e))
        lse_ref[h:h + 1, :] = jnp.transpose(lse)[0:1, :]

    def answer_col(h, r):
        if reach == 2:
            far, close = 1 - inner, inner
            tasks = [
                (far, [row_piece(inner, h), row_piece(1 - inner, h)]),
                (close, [row_piece(inner, h)]),
            ]
            for d, pieces in tasks:
                total, top = partial(q_col[d, rows(r), lanes(h)], outer_of(d) * per + r, pieces)
                answer(total, top, o_col.at[d, rows(r), lanes(h)], lse_col.at[d, r], h)
        else:
            for d in (DOWN, UP):
                low, high = (0, inner + 1) if d == DOWN else (inner, reach)
                total, top = partial_row(
                    q_col[d, rows(r), lanes(h)], outer_of(d) * per + r, h, low, high
                )
                answer(total, top, o_col.at[d, rows(r), lanes(h)], lse_col.at[d, r], h)

    def answer_row(h, r):
        def one(p):
            d = (p > inner).astype(jnp.int32)
            pieces = [row_piece(inner, h), col_piece(d, h)]
            total, top = partial(q_row[p, rows(r), lanes(h)], in_row(p) * per + r, pieces)
            answer(total, top, o_row.at[p, rows(r), lanes(h)], lse_row.at[p, r], h)
        each_peer(one)

    def send_col(h, r):
        each_outer(lambda d: o_col_copy(d, r, h).start())

    def send_row(h, r):
        @pl.when(t >= 0)
        def _():
            each_peer(lambda p: o_row_copy(p, r, h).start())

    def send_lse(r):
        each_outer(lambda d: lse_col_copy(d, r).start())

        @pl.when(t >= 0)
        def _():
            each_peer(lambda p: lse_row_copy(p, r).start())

    def wait_row_keys(h):
        for kind in (K, V):
            each_peer(lambda p: kv_row_copy(p, kind, h, p).wait_recv())

    def wait_col_keys(h):
        def go(d):
            for kind in (K, V):
                kv_col_copy(d, kind, h, d).wait_recv()
        each_outer(go)

    def wait_queries(r):
        each_peer(lambda p: q_row_copy(p, r, 0, p).wait_recv())
        by_core(1, lambda: each_peer(lambda p: q_row_copy(p, r, 1, p).wait_recv()))
        each_outer(lambda d: q_col_copy(d, r, 0, d).wait_recv())
        by_core(0, lambda: each_outer(lambda d: q_col_copy(d, r, 1, d).wait_recv()))

    for copy in own:
        copy.wait()
    wait_queries(0)
    for a, b in zip(row_heads, col_heads):
        wait_row_keys(a)
        wait_col_keys(b)
        answer_col(a, 0)
        answer_row(b, 0)
        own_row(a)
        own_col(b)
        send_col(a, 0)
        send_row(b, 0)

    def middle_row():
        wait_row_keys(middle)
        answer_col(middle, 0)
        send_col(middle, 0)

    def middle_col():
        wait_col_keys(middle)
        answer_row(middle, 0)
        send_row(middle, 0)

    by_core(0, middle_row)
    by_core(1, middle_col)
    send_lse(0)
    by_core(0, lambda: own_row(middle))
    by_core(1, lambda: own_col(middle))

    for r in range(1, per):
        wait_queries(r)
        for a, b in zip(row_heads, col_heads):
            answer_col(a, r)
            answer_row(b, r)
        by_core(0, lambda: answer_col(middle, r))
        by_core(1, lambda: answer_row(middle, r))
        for a, b in zip(row_heads, col_heads):
            send_col(a, r)
            send_row(b, r)
        by_core(0, lambda: send_col(middle, r))
        by_core(1, lambda: send_row(middle, r))
        send_lse(r)

    def spread(row):
        return jnp.transpose(jnp.broadcast_to(row, (BLK, BLK)))

    def merge(h, r, parts):
        total, top = acc[h, rows(r), :], peak[h, rows(r), :]
        logs = [spread(lse) for _, lse in parts]
        best = functools.reduce(jnp.maximum, logs, top)
        scale = jnp.exp2(top - best)
        upper, below = total[:, :HD] * scale, total[:, HD:] * scale
        for (value, _), log in zip(parts, logs):
            weight = jnp.exp2(log - best)
            upper = upper + value.astype(jnp.float32) * weight
            below = below + weight
        return upper, below, best

    def finish(h, r, parts):
        upper, below, _ = merge(h, r, parts)
        att[rows(r), lanes(h)] = (upper * (1.0 / below)).astype(jnp.bfloat16)

    def finish_row(h, r):
        finish(h, r, [
            (got_col[d, rows(r), lanes(h)], got_lse_col[d, r, h:h + 1, :]) for d in (DOWN, UP)
        ])

    def finish_col(h, r):
        def part(p):
            return got_row[p, rows(r), lanes(h)], got_lse_row[p, r, h:h + 1, :]

        if reach == 2:
            finish(h, r, [part(1 - inner)])
        else:
            def fold(p):
                upper, below, best = merge(h, r, [part(p)])
                acc[h, rows(r), :] = jnp.concatenate([upper, below], axis=1)
                peak[h, rows(r), :] = best
            each_peer(fold)
            finish(h, r, [])

    def wait_answers(r):
        for h in row_heads:
            each_outer(lambda d: o_col_copy(d, r, h, d).wait_recv())
        for h in col_heads:
            each_peer(lambda p: o_row_copy(p, r, h, p).wait_recv())
        by_core(0, lambda: each_outer(lambda d: o_col_copy(d, r, middle, d).wait_recv()))
        by_core(1, lambda: each_peer(lambda p: o_row_copy(p, r, middle, p).wait_recv()))
        each_outer(lambda d: lse_col_copy(d, r, d).wait_recv())
        each_peer(lambda p: lse_row_copy(p, r, p).wait_recv())

    def project(jy, r, k):
        part = slice(k * width, (k + 1) * width)
        mine = jnp.dot(att[rows(r), :], w_own[jy, :, part], preferred_element_type=jnp.float32)
        other = jnp.dot(
            att_peer[rows(r), :], w_peer[jy, :, part], preferred_element_type=jnp.float32
        )
        return mine + other

    for copy in weights:
        copy.wait()
    for jy in range(chips):
        weight_copy(jy).wait_recv()
    for r in range(per):
        wait_answers(r)
        by_core(0, lambda: finish_row(middle, r))
        by_core(1, lambda: finish_col(middle, r))
        for a, b in zip(row_heads, col_heads):
            finish_row(a, r)
            finish_col(b, r)

        @pl.when(t >= 0)
        def _():
            att_copy(r).start()
        att_copy(r).wait_recv()
        for jy in range(1, chips):
            for k in range(chunks):
                stage_y[jy - 1, r, k] = project(jy, r, k).astype(jnp.bfloat16)

                @pl.when(t >= 0)
                def _():
                    chip_copy(jy, r, k).start()
        for k in range(chunks):
            near[r, k] = project(0, r, k)
    for r in range(per):
        for k in range(chunks):
            total = near[r, k]
            for jy in range(1, chips):
                chip_copy(chips - jy, r, k).wait_recv()
            for other in range(chips - 1):
                total = total + recv_y[other, r, k].astype(jnp.float32)
            final[r, k] = total.astype(jnp.bfloat16)

            @pl.when(t >= 0)
            def _():
                out_copy(r, k).start()

    for a, b in zip(row_heads, col_heads):
        for kind in (K, V):
            each_peer(lambda p: kv_row_copy(p, kind, a).wait_send())
            each_outer(lambda d: kv_col_copy(d, kind, b).wait_send())
        for r in range(per):
            each_outer(lambda d: o_col_copy(d, r, a).wait_send())
            each_peer(lambda p: o_row_copy(p, r, b).wait_send())

    def middle_row_end():
        for kind in (K, V):
            each_peer(lambda p: kv_row_copy(p, kind, middle).wait_send())
        for r in range(per):
            each_outer(lambda d: o_col_copy(d, r, middle).wait_send())
            each_outer(lambda d: q_col_copy(d, r, 1).wait_send())

    def middle_col_end():
        for kind in (K, V):
            each_outer(lambda d: kv_col_copy(d, kind, middle).wait_send())
        for r in range(per):
            each_peer(lambda p: o_row_copy(p, r, middle).wait_send())
            each_peer(lambda p: q_row_copy(p, r, 1).wait_send())

    by_core(0, middle_row_end)
    by_core(1, middle_col_end)
    for r in range(per):
        each_peer(lambda p: q_row_copy(p, r, 0).wait_send())
        each_outer(lambda d: q_col_copy(d, r, 0).wait_send())
        each_peer(lambda p: lse_row_copy(p, r).wait_send())
        each_outer(lambda d: lse_col_copy(d, r).wait_send())
        att_copy(r).wait_send()
    for jy in range(chips):
        weight_copy(jy).wait_send()
    for r in range(per):
        for k in range(chunks):
            for jy in range(1, chips):
                chip_copy(jy, r, k).wait_send()
            out_copy(r, k).wait()


def shards(count, tp_count, queries, keys, values, block_mask, w_out):
    tok, cols = queries.shape
    heads = cols // HD
    per = tok // BLK
    reach = count // 4
    chips = tp_count // 2
    depth, wide = w_out.shape
    out_cols = wide // tp_count
    chunks = max(1, out_cols // 256)
    width = out_cols // chunks
    bf16, f32 = jnp.bfloat16, jnp.float32
    dma = pltpu.SemaphoreType.DMA
    tall = -(-heads // 8) * 8
    return pl.pallas_call(
        functools.partial(kernel, reach, count, tp_count, chunks),
        out_shape=jax.ShapeDtypeStruct((tok, out_cols), bf16),
        in_specs=[
            pl.BlockSpec(memory_space=pltpu.SMEM),
            pl.BlockSpec(memory_space=pl.ANY),
            pl.BlockSpec(memory_space=pl.ANY),
            pl.BlockSpec(memory_space=pl.ANY),
            pl.BlockSpec(memory_space=pl.ANY),
        ],
        out_specs=pl.BlockSpec(memory_space=pl.ANY),
        scratch_shapes=[
            pltpu.VMEM((tok, cols), bf16),
            pltpu.VMEM((reach, 2, tok, cols), bf16),
            pltpu.VMEM((2, 2, tok, cols), bf16),
            pltpu.VMEM((reach, tok, cols), bf16),
            pltpu.VMEM((2, tok, cols), bf16),
            pltpu.VMEM((reach, tok, cols), bf16),
            pltpu.VMEM((2, tok, cols), bf16),
            pltpu.VMEM((reach, tok, cols), bf16),
            pltpu.VMEM((2, tok, cols), bf16),
            pltpu.VMEM((reach, per, tall, BLK), f32),
            pltpu.VMEM((2, per, tall, BLK), f32),
            pltpu.VMEM((reach, per, tall, BLK), f32),
            pltpu.VMEM((2, per, tall, BLK), f32),
            pltpu.VMEM((heads, tok, 2 * HD), f32),
            pltpu.VMEM((heads, tok, HD), f32),
            pltpu.VMEM((tok, cols), bf16),
            pltpu.VMEM((tok, cols), bf16),
            pltpu.VMEM((chips, depth, out_cols), bf16),
            pltpu.VMEM((chips, depth, out_cols), bf16),
            pltpu.VMEM((chips - 1, per, chunks, BLK, width), bf16),
            pltpu.VMEM((chips - 1, per, chunks, BLK, width), bf16),
            pltpu.VMEM((per, chunks, BLK, width), f32),
            pltpu.VMEM((per, chunks, BLK, width), bf16),
            dma((3,)),
            dma((chips,)),
            dma((chips,)),
            dma((chips,)),
            dma((reach, 2, heads)),
            dma((reach, 2, heads)),
            dma((2, 2, heads)),
            dma((2, 2, heads)),
            dma((reach, per, 2)),
            dma((reach, per, 2)),
            dma((2, per, 2)),
            dma((2, per, 2)),
            dma((reach, per, heads)),
            dma((reach, per, heads)),
            dma((2, per, heads)),
            dma((2, per, heads)),
            dma((reach, per)),
            dma((reach, per)),
            dma((2, per)),
            dma((2, per)),
            dma((per,)),
            dma((per,)),
            dma((chips - 1, per, chunks)),
            dma((chips - 1, per, chunks)),
            dma((per, chunks)),
        ],
        compiler_params=pltpu.CompilerParams(
            collective_id=0, has_side_effects=True, vmem_limit_bytes=60 * 1024 * 1024
        ),
    )(block_mask, queries, keys, values, w_out)


def solution(mesh):
    return jax.shard_map(
        functools.partial(shards, mesh.shape["ctx"], mesh.shape["tp"]),
        mesh=mesh,
        in_specs=(P("ctx", "tp"), P("ctx", "tp"), P("ctx", "tp"), P(), P("tp", None)),
        out_specs=P("ctx", "tp"),
        check_vma=False,
    )
```

```python
import contextlib
import functools
import math

import jax
import jax.numpy as jnp
from jax import lax
from jax.experimental import pallas as pl
from jax.experimental.pallas import tpu as pltpu
from jax.sharding import PartitionSpec as P

HD = 128
BLK = 128
MESH = pl.DeviceIdType.MESH
K, V = 0, 1
DOWN, UP = 0, 1
NONE = -1e30
phase = contextlib.nullcontext


def kernel(
    reach, count, tp_count, chunks,
    mask_hbm, q_ref, k_ref, v_ref, w_ref, out_ref,
    mask_ref, q_own, kv_row, kv_col, q_row, q_col, o_row, o_col, got_row, got_col,
    lse_row, lse_col, got_lse_row, got_lse_col, acc, peak, att, att_peer,
    w_own, w_peer, stage_y, recv_y, near,
    own_sem, w_sem, wp_send, wp_recv, kvr_send, kvr_recv, kvc_send, kvc_recv,
    qr_send, qr_recv, qc_send, qc_recv, or_send, or_recv, oc_send, oc_recv,
    lr_send, lr_recv, lc_send, lc_recv, att_send, att_recv, y_send, y_recv,
):
    tok, cols = q_own.shape
    heads = cols // HD
    per = tok // BLK
    chips = tp_count // 2
    out_cols = out_ref.shape[1]
    width = out_cols // chunks
    half = heads // 2
    odd = heads % 2
    middle = half
    ctx = lax.axis_index("ctx")
    t = lax.axis_index("tp")
    inner = lax.rem(ctx, reach)
    core = lax.rem(t, 2)
    chip = t // 2
    partner = chip * 2 + 1 - core
    factor = jnp.float32(HD ** (-0.5) * math.log2(math.e))

    def tp_of(jy, which):
        return lax.rem(chip + jy, chips) * 2 + which

    def each_peer(fn):
        if reach == 2:
            fn(1 - inner)
        elif reach > 2:
            def step(j, carry):
                fn(lax.rem(inner + j, reach))
                return carry
            lax.fori_loop(1, reach, step, 0)

    def in_row(p):
        return ctx - inner + p

    def outer_of(d):
        return ctx + (2 * d - 1) * reach

    def inside(c):
        return jnp.logical_and(c >= 0, c < count)

    def each_outer(fn):
        for d in (DOWN, UP):
            @pl.when(inside(outer_of(d)))
            def _(d=d):
                fn(d)

    def lanes(h):
        return slice(h * HD, (h + 1) * HD)

    def rows(r):
        return slice(r * BLK, (r + 1) * BLK)

    def remote(src, dst, send, recv, c, tt):
        return pltpu.make_async_remote_copy(
            src_ref=src, dst_ref=dst, send_sem=send, recv_sem=recv,
            device_id=(c, tt), device_id_type=MESH,
        )

    def turn(h):
        return h if h <= middle else heads - 1 - h

    def row_lanes(wide):
        return slice((half if wide else half + odd) * HD, cols)

    def col_lanes(wide):
        return slice(0, (half + odd if wide else half) * HD)

    def kv_row_copy(p, kind, h):
        return remote(
            (k_ref, v_ref)[kind].at[:, lanes(h)], kv_row.at[inner, kind, :, lanes(h)],
            kvr_send.at[p], kvr_recv.at[inner, turn(h)], in_row(p), t,
        )

    def kv_col_copy(d, kind, h):
        return remote(
            (k_ref, v_ref)[kind].at[:, lanes(h)], kv_col.at[1 - d, kind, :, lanes(h)],
            kvc_send.at[d], kvc_recv.at[1 - d, turn(h)], outer_of(d), t,
        )

    def q_row_copy(p, r, wide):
        part = (rows(r), row_lanes(wide))
        return remote(
            q_ref.at[part], q_row.at[(inner,) + part],
            qr_send.at[p], qr_recv.at[inner, r], in_row(p), t,
        )

    def q_col_copy(d, r, wide):
        part = (rows(r), col_lanes(wide))
        return remote(
            q_ref.at[part], q_col.at[(1 - d,) + part],
            qc_send.at[d], qc_recv.at[1 - d, r], outer_of(d), t,
        )

    def o_row_copy(p, r, h):
        part = (rows(r), lanes(h))
        return remote(
            o_row.at[(p,) + part], got_row.at[(inner,) + part],
            or_send.at[p], or_recv.at[inner, r], in_row(p), t,
        )

    def o_col_copy(d, r, h):
        part = (rows(r), lanes(h))
        return remote(
            o_col.at[(d,) + part], got_col.at[(1 - d,) + part],
            oc_send.at[d], oc_recv.at[1 - d, r], outer_of(d), t,
        )

    def lse_row_copy(p, r):
        return remote(
            lse_row.at[p, r], got_lse_row.at[inner, r],
            lr_send.at[p], lr_recv.at[inner, r], in_row(p), t,
        )

    def lse_col_copy(d, r):
        return remote(
            lse_col.at[d, r], got_lse_col.at[1 - d, r],
            lc_send.at[d], lc_recv.at[1 - d, r], outer_of(d), t,
        )

    def arrived(ref, sem):
        remote(ref, ref, wp_send.at[0], sem, ctx, partner).wait_recv()

    def sent(ref, sem):
        remote(ref, ref, sem, wp_recv.at[0], ctx, partner).wait_send()

    def weight_copy(jy):
        start = pl.multiple_of(tp_of(jy, 1 - core) * out_cols, out_cols)
        return remote(
            w_ref.at[:, pl.ds(start, out_cols)], w_peer.at[jy],
            wp_send.at[0], wp_recv.at[jy], ctx, partner,
        )

    def att_copy(r):
        return remote(
            att.at[rows(r), :], att_peer.at[rows(r), :],
            att_send.at[0], att_recv.at[r], ctx, partner,
        )

    def chip_copy(jy, r, k):
        return remote(
            stage_y.at[jy - 1, r, k], recv_y.at[chips - jy - 1, r, k],
            y_send.at[0], y_recv.at[chips - jy - 1, r, k], ctx, tp_of(jy, core),
        )

    own = [
        pltpu.make_async_copy(mask_hbm, mask_ref, own_sem.at[3]),
        pltpu.make_async_copy(q_ref, q_own, own_sem.at[0]),
        pltpu.make_async_copy(k_ref, kv_row.at[inner, K], own_sem.at[1]),
        pltpu.make_async_copy(v_ref, kv_row.at[inner, V], own_sem.at[2]),
    ]
    weights = []
    for jy in range(chips):
        start = pl.multiple_of(tp_of(jy, core) * out_cols, out_cols)
        weights.append(pltpu.make_async_copy(
            w_ref.at[:, pl.ds(start, out_cols)], w_own.at[jy], w_sem.at[jy]
        ))

    for copy in own:
        copy.start()
    barrier = pltpu.get_barrier_semaphore()

    def greet(c, tt):
        pl.semaphore_signal(barrier, inc=1, device_id=(c, tt), device_id_type=MESH)

    with phase("bar"):
        each_peer(lambda p: greet(in_row(p), t))
        each_outer(lambda d: greet(outer_of(d), t))
        greet(ctx, partner)
        for jy in range(1, chips):
            greet(ctx, tp_of(jy, core))
        outer_count = inside(outer_of(DOWN)).astype(jnp.int32) + inside(outer_of(UP)).astype(jnp.int32)
        pl.semaphore_wait(barrier, reach - 1 + 1 + chips - 1 + outer_count)

    row_heads = list(range(half))
    col_heads = list(range(heads - 1, heads - 1 - half, -1))

    def by_core(which, fn):
        if odd:
            @pl.when(core == which)
            def _():
                fn()

    def each_core(fn):
        if odd:
            for which in (0, 1):
                by_core(which, lambda which=which: fn(which == 1, which == 0))
        else:
            fn(False, False)

    def start_queries(r):
        def go(row_wide, col_wide):
            each_peer(lambda p: q_row_copy(p, r, row_wide).start())
            each_outer(lambda d: q_col_copy(d, r, col_wide).start())
        each_core(go)

    def start_row_keys(h):
        for kind in (K, V):
            each_peer(lambda p: kv_row_copy(p, kind, h).start())

    def start_col_keys(h):
        def go(d):
            for kind in (K, V):
                kv_col_copy(d, kind, h).start()
        each_outer(go)

    with phase("starts"):
        start_queries(0)
        for a, b in zip(row_heads, col_heads):
            start_row_keys(a)
            start_col_keys(b)
        by_core(0, lambda: start_row_keys(middle))
        by_core(1, lambda: start_col_keys(middle))
        for r in range(1, per):
            start_queries(r)

    for d in (DOWN, UP):
        @pl.when(jnp.logical_not(inside(outer_of(d))))
        def _(d=d):
            kv_col[d] = jnp.zeros(kv_col.shape[1:], kv_col.dtype)
            q_col[d] = jnp.zeros(q_col.shape[1:], q_col.dtype)
            got_col[d] = jnp.zeros(got_col.shape[1:], got_col.dtype)
            got_lse_col[d] = jnp.full(got_lse_col.shape[1:], NONE, jnp.float32)
    lse_row[...] = jnp.zeros_like(lse_row)
    lse_col[...] = jnp.zeros_like(lse_col)

    def bias_of(block, owner):
        owner_in = jnp.clip(owner, 0, count - 1)
        block_in = jnp.clip(block, 0, count * per - 1)
        parts = []
        for b in range(per):
            flag = jnp.where(inside(owner), mask_ref[block_in, owner_in * per + b], 0)
            value = jnp.where(flag > 0, jnp.float32(0.0), jnp.float32(NONE))
            parts.append(jnp.full((1, BLK), value, jnp.float32))
        return parts

    def scores_of(query, pieces):
        key = jnp.concatenate([piece[0] for piece in pieces], axis=0)
        return lax.dot_general(
            query, key, (((1,), (1,)), ((), ())), preferred_element_type=jnp.float32
        )

    def sums_of(weight, pieces):
        value = jnp.concatenate([piece[1] for piece in pieces], axis=0)
        ones = jnp.ones((value.shape[0], HD), jnp.bfloat16)
        return jnp.dot(
            weight, jnp.concatenate([value, ones], axis=1), preferred_element_type=jnp.float32
        )

    def partial(query, block, pieces):
        raw = scores_of(query, pieces)
        weight, tops = [], []
        for a in range(query.shape[0] // BLK):
            bias = jnp.concatenate(
                sum([bias_of(block + a, piece[2]) for piece in pieces], []), axis=1
            )
            scores = raw[rows(a)] + bias
            top = jnp.broadcast_to(jnp.max(scores, axis=1, keepdims=True), (BLK, HD))
            wide = jnp.concatenate([top] * (scores.shape[1] // HD), axis=1)
            weight.append(jnp.exp2((scores - wide) * factor).astype(jnp.bfloat16))
            tops.append(top * factor)
        return sums_of(jnp.concatenate(weight, axis=0), pieces), jnp.concatenate(tops, axis=0)

    def fade(before, after):
        scale = jnp.exp2(before - after)
        return jnp.concatenate([scale, scale], axis=1)

    def partial_row(query, block, h, low, high):
        def step(slot, carry):
            total, top = carry
            more, more_top = partial(query, block, [row_piece(slot, h)])
            best = jnp.maximum(top, more_top)
            return total * fade(top, best) + more * fade(more_top, best), best
        shape = (query.shape[0], HD)
        first = (jnp.zeros((shape[0], 2 * HD), jnp.float32), jnp.full(shape, -1e38, jnp.float32))
        return lax.fori_loop(low, high, step, first)

    def row_piece(slot, h):
        return kv_row[slot, K, :, lanes(h)], kv_row[slot, V, :, lanes(h)], in_row(slot)

    def col_piece(d, h):
        return kv_col[d, K, :, lanes(h)], kv_col[d, V, :, lanes(h)], outer_of(d)

    def keep(h, total, top):
        acc[h] = total
        peak[h] = top

    def own_row(h):
        query = q_own[:, lanes(h)]
        if reach == 2:
            pieces = [row_piece(inner, h), row_piece(1 - inner, h)]
            keep(h, *partial(query, ctx * per, pieces))
        else:
            keep(h, *partial_row(query, ctx * per, h, 0, reach))

    def own_col(h):
        pieces = [row_piece(inner, h), col_piece(DOWN, h), col_piece(UP, h)]
        keep(h, *partial(q_own[:, lanes(h)], ctx * per, pieces))

    def answer(total, top, o_ref, lse_ref, h):
        below = total[:, HD:]
        o_ref[...] = (total[:, :HD] * (1.0 / below)).astype(jnp.bfloat16)
        lse = top + jnp.log(below) * jnp.float32(math.log2(math.e))
        lse_ref[h:h + 1, :] = jnp.transpose(lse)[0:1, :]

    def answer_col(h, r):
        if reach == 2:
            far, close = 1 - inner, inner
            tasks = [
                (far, [row_piece(inner, h), row_piece(1 - inner, h)]),
                (close, [row_piece(inner, h)]),
            ]
            for d, pieces in tasks:
                total, top = partial(q_col[d, rows(r), lanes(h)], outer_of(d) * per + r, pieces)
                answer(total, top, o_col.at[d, rows(r), lanes(h)], lse_col.at[d, r], h)
        else:
            for d in (DOWN, UP):
                low, high = (0, inner + 1) if d == DOWN else (inner, reach)
                total, top = partial_row(
                    q_col[d, rows(r), lanes(h)], outer_of(d) * per + r, h, low, high
                )
                answer(total, top, o_col.at[d, rows(r), lanes(h)], lse_col.at[d, r], h)

    def answer_row(h, r):
        def one(p):
            d = (p > inner).astype(jnp.int32)
            pieces = [row_piece(inner, h), col_piece(d, h)]
            total, top = partial(q_row[p, rows(r), lanes(h)], in_row(p) * per + r, pieces)
            answer(total, top, o_row.at[p, rows(r), lanes(h)], lse_row.at[p, r], h)
        each_peer(one)

    def send_col(h, r):
        each_outer(lambda d: o_col_copy(d, r, h).start())

    def send_row(h, r):
        @pl.when(t >= 0)
        def _():
            each_peer(lambda p: o_row_copy(p, r, h).start())

    def send_lse(r):
        each_outer(lambda d: lse_col_copy(d, r).start())

        @pl.when(t >= 0)
        def _():
            each_peer(lambda p: lse_row_copy(p, r).start())

    def wait_row_keys(h):
        each_peer(lambda p: arrived(kv_row.at[p, :, :, lanes(h)], kvr_recv.at[p, turn(h)]))

    def wait_col_keys(h):
        each_outer(lambda d: arrived(kv_col.at[d, :, :, lanes(h)], kvc_recv.at[d, turn(h)]))

    def wait_queries(r):
        def go(row_wide, col_wide):
            each_peer(lambda p: arrived(
                q_row.at[p, rows(r), row_lanes(row_wide)], qr_recv.at[p, r]))
            each_outer(lambda d: arrived(
                q_col.at[d, rows(r), col_lanes(col_wide)], qc_recv.at[d, r]))
        each_core(go)

    with phase("waitown"):
        for copy in own:
            copy.wait()
    with phase("waitq"):
        wait_queries(0)
    for jy in list(range(1, chips)) + [0]:
        weight_copy(jy).start()
    for copy in weights[1:] + weights[:1]:
        copy.start()
    for a, b in zip(row_heads, col_heads):
        with phase("waitkv"):
            wait_row_keys(a)
            wait_col_keys(b)
        with phase("step"):
            answer_col(a, 0)
            answer_row(b, 0)
            own_row(a)
            own_col(b)
            send_col(a, 0)
            send_row(b, 0)

    def middle_row():
        with phase("mwaitkv"):
            wait_row_keys(middle)
        answer_col(middle, 0)
        send_col(middle, 0)

    def middle_col():
        with phase("mwaitkv"):
            wait_col_keys(middle)
        answer_row(middle, 0)
        send_row(middle, 0)

    with phase("mid"):
        by_core(0, middle_row)
        by_core(1, middle_col)
        send_lse(0)
    with phase("ownmid"):
        by_core(0, lambda: own_row(middle))
        by_core(1, lambda: own_col(middle))

    for r in range(1, per):
        with phase("waitq1"):
            wait_queries(r)
        with phase("answer1"):
            for a, b in zip(row_heads, col_heads):
                answer_col(a, r)
                answer_row(b, r)
            by_core(0, lambda: answer_col(middle, r))
            by_core(1, lambda: answer_row(middle, r))
            for a, b in zip(row_heads, col_heads):
                send_col(a, r)
                send_row(b, r)
            by_core(0, lambda: send_col(middle, r))
            by_core(1, lambda: send_row(middle, r))
            send_lse(r)

    def spread(row):
        return jnp.transpose(jnp.broadcast_to(row, (BLK, BLK)))

    def merge(h, r, parts):
        total, top = acc[h, rows(r), :], peak[h, rows(r), :]
        logs = [spread(lse) for _, lse in parts]
        best = functools.reduce(jnp.maximum, logs, top)
        scale = jnp.exp2(top - best)
        upper, below = total[:, :HD] * scale, total[:, HD:] * scale
        for (value, _), log in zip(parts, logs):
            weight = jnp.exp2(log - best)
            upper = upper + value.astype(jnp.float32) * weight
            below = below + weight
        return upper, below, best

    def finish(h, r, parts):
        upper, below, _ = merge(h, r, parts)
        att[rows(r), lanes(h)] = (upper * (1.0 / below)).astype(jnp.bfloat16)

    def finish_row(h, r):
        finish(h, r, [
            (got_col[d, rows(r), lanes(h)], got_lse_col[d, r, h:h + 1, :]) for d in (DOWN, UP)
        ])

    def finish_col(h, r):
        def part(p):
            return got_row[p, rows(r), lanes(h)], got_lse_row[p, r, h:h + 1, :]

        if reach == 2:
            finish(h, r, [part(1 - inner)])
        else:
            def fold(p):
                upper, below, best = merge(h, r, [part(p)])
                acc[h, rows(r), :] = jnp.concatenate([upper, below], axis=1)
                peak[h, rows(r), :] = best
            each_peer(fold)
            finish(h, r, [])

    def wait_answers(r):
        def go(row_wide, col_wide):
            each_peer(lambda p: arrived(
                got_row.at[p, rows(r), row_lanes(row_wide)], or_recv.at[p, r]))
            each_outer(lambda d: arrived(
                got_col.at[d, rows(r), col_lanes(col_wide)], oc_recv.at[d, r]))
        each_core(go)
        each_outer(lambda d: arrived(got_lse_col.at[d, r], lc_recv.at[d, r]))
        each_peer(lambda p: arrived(got_lse_row.at[p, r], lr_recv.at[p, r]))

    def project(jy, r, k):
        part = slice(k * width, (k + 1) * width)
        mine = jnp.dot(att[rows(r), :], w_own[jy, :, part], preferred_element_type=jnp.float32)
        other = jnp.dot(
            att_peer[rows(r), :], w_peer[jy, :, part], preferred_element_type=jnp.float32
        )
        return mine + other

    with phase("waitw"):
        for copy in weights:
            copy.wait()
        for jy in range(chips):
            weight_copy(jy).wait_recv()
    for r in range(per):
        with phase("waitans"):
            wait_answers(r)
        with phase("finish"):
            by_core(0, lambda: finish_row(middle, r))
            by_core(1, lambda: finish_col(middle, r))
            for a, b in zip(row_heads, col_heads):
                finish_row(a, r)
                finish_col(b, r)

            @pl.when(t >= 0)
            def _():
                att_copy(r).start()
        with phase("waitatt"):
            att_copy(r).wait_recv()
        with phase("far"):
            for jy in range(1, chips):
                for k in range(chunks):
                    stage_y[jy - 1, r, k] = project(jy, r, k).astype(jnp.bfloat16)

                    @pl.when(t >= 0)
                    def _():
                        chip_copy(jy, r, k).start()
        with phase("near"):
            for k in range(chunks):
                near[r, k] = project(0, r, k)
    with phase("final"):
        for r in range(per):
            for k in range(chunks):
                total = near[r, k]
                for jy in range(1, chips):
                    chip_copy(chips - jy, r, k).wait_recv()
                for other in range(chips - 1):
                    total = total + recv_y[other, r, k].astype(jnp.float32)
                out_ref[rows(r), k * width:(k + 1) * width] = total.astype(jnp.bfloat16)

    with phase("tail"):
        def go(row_wide, col_wide):
            def row_sent(p):
                sent(kv_row.at[p, :, :, col_lanes(col_wide)], kvr_send.at[p])
                sent(q_row.at[p, :, row_lanes(row_wide)], qr_send.at[p])
                sent(o_row.at[p, :, row_lanes(row_wide)], or_send.at[p])
                sent(lse_row.at[p], lr_send.at[p])

            def col_sent(d):
                sent(kv_col.at[d, :, :, row_lanes(row_wide)], kvc_send.at[d])
                sent(q_col.at[d, :, col_lanes(col_wide)], qc_send.at[d])
                sent(o_col.at[d, :, col_lanes(col_wide)], oc_send.at[d])
                sent(lse_col.at[d], lc_send.at[d])

            each_peer(row_sent)
            each_outer(col_sent)
        each_core(go)
        sent(att, att_send.at[0])
        sent(w_peer, wp_send.at[0])
        sent(stage_y, y_send.at[0])


def shards(count, tp_count, queries, keys, values, block_mask, w_out):
    tok, cols = queries.shape
    heads = cols // HD
    per = tok // BLK
    reach = count // 4
    chips = tp_count // 2
    depth, wide = w_out.shape
    out_cols = wide // tp_count
    chunks = max(1, out_cols // 256)
    width = out_cols // chunks
    bf16, f32 = jnp.bfloat16, jnp.float32
    dma = pltpu.SemaphoreType.DMA
    tall = -(-heads // 8) * 8
    turns = heads // 2 + heads % 2
    return pl.pallas_call(
        functools.partial(kernel, reach, count, tp_count, chunks),
        out_shape=pltpu.VMEM((tok, out_cols), bf16),
        in_specs=[
            pl.BlockSpec(memory_space=pltpu.HBM),
            pl.BlockSpec(memory_space=pltpu.HBM),
            pl.BlockSpec(memory_space=pltpu.HBM),
            pl.BlockSpec(memory_space=pltpu.HBM),
            pl.BlockSpec(memory_space=pltpu.HBM),
        ],
        out_specs=pl.BlockSpec(memory_space=pltpu.VMEM),
        scratch_shapes=[
            pltpu.SMEM(block_mask.shape, block_mask.dtype),
            pltpu.VMEM((tok, cols), bf16),
            pltpu.VMEM((reach, 2, tok, cols), bf16),
            pltpu.VMEM((2, 2, tok, cols), bf16),
            pltpu.VMEM((reach, tok, cols), bf16),
            pltpu.VMEM((2, tok, cols), bf16),
            pltpu.VMEM((reach, tok, cols), bf16),
            pltpu.VMEM((2, tok, cols), bf16),
            pltpu.VMEM((reach, tok, cols), bf16),
            pltpu.VMEM((2, tok, cols), bf16),
            pltpu.VMEM((reach, per, tall, BLK), f32),
            pltpu.VMEM((2, per, tall, BLK), f32),
            pltpu.VMEM((reach, per, tall, BLK), f32),
            pltpu.VMEM((2, per, tall, BLK), f32),
            pltpu.VMEM((heads, tok, 2 * HD), f32),
            pltpu.VMEM((heads, tok, HD), f32),
            pltpu.VMEM((tok, cols), bf16),
            pltpu.VMEM((tok, cols), bf16),
            pltpu.VMEM((chips, depth, out_cols), bf16),
            pltpu.VMEM((chips, depth, out_cols), bf16),
            pltpu.VMEM((chips - 1, per, chunks, BLK, width), bf16),
            pltpu.VMEM((chips - 1, per, chunks, BLK, width), bf16),
            pltpu.VMEM((per, chunks, BLK, width), f32),
            dma((4,)),
            dma((chips,)),
            dma((1,)),
            dma((chips,)),
            dma((reach,)),
            dma((reach, turns)),
            dma((2,)),
            dma((2, turns)),
            dma((reach,)),
            dma((reach, per)),
            dma((2,)),
            dma((2, per)),
            dma((reach,)),
            dma((reach, per)),
            dma((2,)),
            dma((2, per)),
            dma((reach,)),
            dma((reach, per)),
            dma((2,)),
            dma((2, per)),
            dma((1,)),
            dma((per,)),
            dma((1,)),
            dma((chips - 1, per, chunks)),
        ],
        compiler_params=pltpu.CompilerParams(
            collective_id=0, has_side_effects=True, vmem_limit_bytes=56 * 1024 * 1024
        ),
    )(block_mask, queries, keys, values, w_out)


def solution(mesh):
    return jax.shard_map(
        functools.partial(shards, mesh.shape["ctx"], mesh.shape["tp"]),
        mesh=mesh,
        in_specs=(P("ctx", "tp"), P("ctx", "tp"), P("ctx", "tp"), P(), P("tp", None)),
        out_specs=P("ctx", "tp"),
        check_vma=False,
    )
```
